32 devices in a mesh: enc: 4 (over y, x), dec: 4 (over z), ret: 2 (over core).
Axes of the slice: x: 2, y: 2, z: 4, core: 2. Of those that a mesh axis runs over, the one named last changes fastest.
Arguments:
- enc_states: bfloat16 [8, 2, 256, 4096], P('enc', 'ret'), may hold values from -22 to 22
- kv_weight: bfloat16 [4096, 64, 128], P(None, 'dec'), may hold values from -1 to 1
- queries: bfloat16 [2, 128, 64, 64], P('ret', None, ('dec', 'enc')), may hold values from -47 to 47
- out_grad: bfloat16 [2, 128, 64, 64], P('ret', None, ('dec', 'enc')), may hold values from -6 to 6
- passage_order: int32 [2, 8], P('ret'), may hold values from 0 to 7, each once within a row
- passage_blocks: int32 [2, 8], P('ret'), may hold values from 1 to 2
- ret_tokens: bfloat16 [8, 2, 256, 768], P('enc', 'ret'), may hold values from -6 to 6
- ret_weight: bfloat16 [768, 768], replicated, may hold values from -0.21875 to 0.21875
- question_emb: float32 [2, 768], P('ret'), may hold values from -7 to 7
Outputs:
- kv_grad: bfloat16 [8, 2, 256, 64, 128], P('enc', 'ret', None, 'dec')
- kv_weight_grad: bfloat16 [4096, 64, 128], P(('enc', 'ret'), 'dec')
- ret_weight_grad: bfloat16 [768, 768], replicated
The draws below stay inside these ranges and needn't reach their ends.
Inputs may be any that keep to these rules, and one draw needn't show every extreme that they name: `passage_order`: each row lists every passage of its group once; slots i * 8 to (i + 1) * 8 - 1 belong to question i of the group.
All inputs are finite; a program needn't handle non-finite values.
Results may differ from the reference program's by a relative error of at most 0.025.
Values may be sent and summed in bfloat16 or wider, within the bound.
A program may use at most 128 MiB of HBM per device.

```python
import math
import jax
import jax.numpy as jnp
from jax import lax

D = 4096
HEADS = 64
HD = 64
RD = 768
BLK = 128
MAXB = 2
PASS = 8
P_DEV = 2
LQ = 128
SLOT = 256
GP = 8
QG = 1
QUESTIONS = 2
N_ENC = 4
N_RET = 2


def shared_directions(key):
    along_model = jnp.clip(jax.random.normal(jax.random.fold_in(key, 9101), (D,), jnp.float32), -3.0, 3.0)
    along_head = jnp.clip(jax.random.normal(jax.random.fold_in(key, 9102), (HEADS, HD), jnp.float32), -3.0, 3.0)
    return (along_model, along_head)


def draw_enc_states(key, part):
    along_model, along_head = shared_directions(key)
    noise_key = jax.random.fold_in(key, 9201)
    noise = jnp.clip(jax.random.normal(noise_key, (GP, N_RET, SLOT, D), jnp.float32), -4.5, 4.5)
    enc_blocks = GP // P_DEV
    pairing = jax.random.permutation(jax.random.fold_in(key, 9202), enc_blocks)
    passage_block = jnp.arange(GP, dtype=jnp.int32) // P_DEV
    width_block = jnp.arange(D, dtype=jnp.int32) // (D // enc_blocks)
    matched = pairing[passage_block][:, None] == width_block[None, :]
    boost = jnp.where(matched, 3.0, 1.0).astype(jnp.float32)[:, None, None, :]
    passage_offset = jax.random.uniform(jax.random.fold_in(key, 9204), (GP, N_RET, 1, 1), jnp.float32, -1.5, 1.5)
    return (noise * boost + (1.0 + passage_offset) * along_model[None, None, None, :]).astype(jnp.bfloat16)


def draw_kv_weight(key, part):
    along_model, along_head = shared_directions(key)
    noise_key = jax.random.fold_in(key, 9251)
    noise = jnp.clip(jax.random.normal(noise_key, (D, HEADS, 2 * HD), jnp.float32), -5.0, 5.0)
    noise = noise / jnp.sqrt(jnp.float32(D))
    key_common = 2.0 * along_model[:, None, None] * along_head[None, :, :] / D
    common = jnp.concatenate([key_common, jnp.zeros((D, HEADS, HD), jnp.float32)], axis=-1)
    return (noise + common).astype(jnp.bfloat16)


def draw_queries(key, part):
    along_model, along_head = shared_directions(key)
    noise_key = jax.random.fold_in(key, 9301)
    noise = jnp.clip(jax.random.normal(noise_key, (QUESTIONS, LQ, HEADS, HD), jnp.float32), -4.5, 4.5)
    head_pick = jax.random.randint(jax.random.fold_in(key, 9302), (QUESTIONS,), 0, HEADS)
    ranking = jax.random.permutation(jax.random.fold_in(key, 9303), QUESTIONS)
    levels = jnp.array([14.0, 10.0, 7.0], jnp.float32)
    strength = levels[ranking % 3]
    picked = (jnp.arange(HEADS, dtype=jnp.int32)[None, :] == head_pick[:, None]).astype(jnp.float32) * strength[:, None]
    lifted = picked[:, None, :, None] * along_head[None, None, :, :]
    return (noise + lifted).astype(jnp.bfloat16)


def draw_question_emb(key, part):
    noise_key = jax.random.fold_in(key, 9401)
    noise = jnp.clip(jax.random.normal(noise_key, (QUESTIONS, RD), jnp.float32), -4.5, 4.5)
    ranking = jax.random.permutation(jax.random.fold_in(key, 9402), QUESTIONS)
    lifted_count = max(1, QUESTIONS * 3 // 8)
    levels = jnp.array([1.8, 1.1, 0.6], jnp.float32)
    lift = jnp.where(ranking < lifted_count, levels[ranking % 3], 0.0)
    return (noise + lift[:, None]).astype(jnp.float32)


def plant(values, own_key, smallest, high):
    dims = values.shape
    spot = [jax.random.randint(jax.random.fold_in(own_key, axis), (), 0, dims[axis]) for axis in range(len(dims))]
    values = values.at[tuple(spot)].set(smallest)
    longest = dims.index(max(dims))
    spot[longest] = (spot[longest] + 1) % dims[longest]
    return values.at[tuple(spot)].set(high)


def shard_levels(rng, shape, shards, low, top_value):
    loudness, own = 1.0, jax.random.fold_in(rng, 6)
    for position, parts in shards:
        steps = jnp.exp(jax.random.uniform(jax.random.fold_in(own, position), (parts,), jnp.float32, low / len(shards), top_value / len(shards)))
        loudness = loudness * jnp.repeat(steps, shape[position] // parts).reshape([-1 if axis == position else 1 for axis in range(len(shape))])
    return loudness


def bell_draw(rng, dims, width, bound, split=(), kind=jnp.bfloat16):
    entries = width * jax.random.normal(rng, dims, jnp.float32)
    if split:
        entries = entries * shard_levels(rng, dims, split, -0.22, 0.18)
    return jnp.clip(entries, -bound, bound).astype(kind)


def setup_inputs(seed: int = 0) -> dict:
    key_of = jax.random.split(jax.random.key(seed), 10)
    return {
        "enc_states": draw_enc_states(jax.random.fold_in(key_of[9], 71), 0),
        "kv_weight": draw_kv_weight(jax.random.fold_in(key_of[9], 71), 0),
        "queries": draw_queries(jax.random.fold_in(key_of[9], 71), 0),
        "out_grad": bell_draw(key_of[3], (QUESTIONS, LQ, HEADS, HD), 1.0, 6.0, ((0, 2), (2, 16))),
        "passage_order": jax.vmap(lambda own: jax.random.permutation(own, GP))(jax.random.split(key_of[4], N_RET)).reshape((N_RET, GP)).astype(jnp.int32),
        "passage_blocks": plant(jax.random.randint(key_of[5], (N_RET, GP), 1, MAXB + 1), jax.random.fold_in(key_of[5], 1), 1, MAXB).astype(jnp.int32),
        "ret_tokens": bell_draw(key_of[6], (GP, N_RET, SLOT, RD), 1.0, 6.0, ((0, 4), (1, 2))),
        "ret_weight": bell_draw(key_of[7], (RD, RD), RD ** -0.5, 0.21875),
        "question_emb": draw_question_emb(jax.random.fold_in(key_of[9], 71), 0),
    }


def gelu_grad(pre_act, upstream):
    return jax.vjp(jax.nn.gelu, pre_act)[1](upstream)[0]

def reference(enc_states, kv_weight, queries, out_grad, passage_order, passage_blocks, ret_tokens, ret_weight, question_emb):
    key_value = jnp.dot(enc_states.reshape(-1, D), kv_weight.reshape(D, HEADS * 2 * HD), preferred_element_type=jnp.float32)
    key_value = key_value.reshape(GP, N_RET, SLOT, HEADS, 2 * HD)
    positions = jnp.arange(SLOT, dtype=jnp.int32)
    live = positions[None, None, :] < BLK * jnp.transpose(passage_blocks)[:, :, None]
    order_rows = passage_order.reshape(QUESTIONS, PASS)
    group_rows = jnp.broadcast_to((jnp.arange(QUESTIONS, dtype=jnp.int32) // QG)[:, None], (QUESTIONS, PASS))
    scale = 1.0 / math.sqrt(HD)
    highest = lax.Precision.HIGHEST

    def per_question(number):
        group = number // QG
        chosen = order_rows[number]
        rows_kv = key_value[chosen, group].reshape(PASS * SLOT, HEADS, 2 * HD)
        live_keys = live[chosen, group].reshape(PASS * SLOT)
        keys = rows_kv[:, :, :HD]
        values = rows_kv[:, :, HD:]
        query_one = queries[number].astype(jnp.float32)
        grad_one = out_grad[number].astype(jnp.float32)
        scores = jnp.einsum('lhc,khc->hlk', query_one, keys, precision=highest) * scale
        masked = jnp.where(live_keys[None, None, :], scores, -1e+30)
        top = lax.optimization_barrier(jnp.max(masked, axis=-1, keepdims=True))
        expo = jnp.where(live_keys[None, None, :], jnp.exp(masked - top), 0.0)
        probs = expo / lax.optimization_barrier(jnp.sum(expo, axis=-1, keepdims=True))
        probs_low = probs.astype(jnp.bfloat16).astype(jnp.float32)
        attended = jnp.einsum('hlk,khc->lhc', probs_low, values, precision=highest)
        value_grad = jnp.einsum('hlk,lhc->khc', probs_low, grad_one)
        prob_grad = jnp.einsum('lhc,khc->hlk', grad_one, values, precision=highest)
        row_dot = jnp.einsum('lhc,lhc->hl', grad_one, attended)
        score_grad = (probs * (prob_grad - row_dot[:, :, None]) * scale).astype(jnp.bfloat16).astype(jnp.float32)
        key_grad = jnp.einsum('hlk,lhc->khc', score_grad, query_one)
        pair_grad = jnp.concatenate([key_grad, value_grad], axis=-1).astype(jnp.bfloat16)
        mass = lax.optimization_barrier(jnp.sum(probs, axis=(0, 1))).reshape(PASS, SLOT).sum(axis=-1) / (HEADS * LQ)
        return (pair_grad.reshape(PASS, SLOT, HEADS, 2 * HD), mass)
    grads_all, passage_mass = lax.map(per_question, jnp.arange(QUESTIONS, dtype=jnp.int32))
    kv_grad = jnp.zeros((GP, N_RET, SLOT, HEADS, 2 * HD), jnp.bfloat16).at[order_rows, group_rows].set(grads_all)
    states_blocks = enc_states.reshape(N_ENC, P_DEV, N_RET, SLOT, D)
    grad_blocks = kv_grad.reshape(N_ENC, P_DEV, N_RET, SLOT, HEADS * 2 * HD)

    def add_block(total, number):
        enc_part = number // N_RET
        ret_part = number % N_RET
        rows_left = states_blocks[enc_part][:, ret_part].reshape(P_DEV * SLOT, D)
        rows_right = grad_blocks[enc_part][:, ret_part].reshape(P_DEV * SLOT, HEADS * 2 * HD)
        partial_value = lax.dot_general(rows_left, rows_right, (((0,), (0,)), ((), ())), preferred_element_type=jnp.float32)
        return (total + lax.optimization_barrier(partial_value.astype(jnp.bfloat16)).astype(jnp.float32), None)
    weight_total, unused = lax.scan(add_block, jnp.zeros((D, HEADS * 2 * HD), jnp.float32), jnp.arange(N_ENC * N_RET, dtype=jnp.int32))
    kv_weight_grad = weight_total.astype(jnp.bfloat16).reshape(D, HEADS, 2 * HD)
    pre_act = jnp.dot(ret_tokens.reshape(-1, RD), ret_weight, preferred_element_type=jnp.float32).reshape(GP, N_RET, SLOT, RD)
    hidden = jax.nn.gelu(pre_act)
    lengths = (BLK * jnp.transpose(passage_blocks)).astype(jnp.float32)
    embed = lax.optimization_barrier(jnp.sum(jnp.where(live[..., None], hidden, 0.0), axis=2)) / lengths[..., None]
    chosen_embed = embed[order_rows, group_rows]
    ret_scores = lax.optimization_barrier(jnp.sum(question_emb[:, None, :] * chosen_embed, axis=-1))
    top_score = lax.optimization_barrier(jnp.max(ret_scores, axis=-1, keepdims=True))
    expo_score = jnp.exp(ret_scores - top_score)
    score_gap = expo_score / lax.optimization_barrier(jnp.sum(expo_score, axis=-1, keepdims=True)) - passage_mass
    gap_rows = score_gap[..., None] * question_emb[:, None, :]
    embed_grad = jnp.zeros((GP, N_RET, RD), jnp.float32).at[order_rows, group_rows].set(gap_rows)
    hidden_grad = jnp.where(live[..., None], (embed_grad / lengths[..., None])[:, :, None, :], 0.0)
    pre_grad = gelu_grad(pre_act, hidden_grad).astype(jnp.bfloat16)
    ret_weight_grad = lax.dot_general(ret_tokens.reshape(-1, RD), pre_grad.reshape(-1, RD), (((0,), (0,)), ((), ())), preferred_element_type=jnp.float32)
    return (kv_grad, kv_weight_grad, ret_weight_grad.astype(jnp.bfloat16))
```

```python
import functools
import math

import jax
import jax.numpy as jnp
from jax import lax
from jax.experimental import pallas as pl
from jax.experimental.pallas import tpu as pltpu
from jax.sharding import PartitionSpec as P

HEADS = 64
BLK = 128
PASS = 8


def gelu_grad(pre_act, upstream):
    return jax.vjp(jax.nn.gelu, pre_act)[1](upstream)[0]


def project_kernel(heads_here, x_ref, w_ref, out_ref, total):
    step = pl.program_id(0)
    heads = w_ref.shape[1]
    pair = w_ref.shape[2]
    head_dim = pair // 2
    x = x_ref[...]
    for first in range(0, heads, 2):
        w_two = jnp.concatenate([w_ref[:, first, :], w_ref[:, first + 1, :]], axis=-1)
        part = jnp.dot(x, w_two, preferred_element_type=jnp.float32)
        cols = slice(first * pair, (first + 2) * pair)

        @pl.when(step == 0)
        def _():
            total[:, cols] = part

        @pl.when(step > 0)
        def _():
            total[:, cols] += part

    @pl.when(step == pl.num_programs(0) - 1)
    def _():
        for h in range(heads):
            dest, own = h // heads_here, h % heads_here
            wide = total[:, h * pair : (h + 1) * pair]
            high = wide.astype(jnp.bfloat16)
            low = (wide - high.astype(jnp.float32)).astype(jnp.bfloat16)
            out_ref[dest, :, own * pair : (own + 1) * pair] = high
            start = heads_here * pair + own * head_dim
            out_ref[dest, :, start : start + head_dim] = low[:, :head_dim]


def project(tok_rows, kv_weight, shards):
    rows, width = tok_rows.shape
    _, heads, pair = kv_weight.shape
    heads_here = heads // shards
    depth = min(512, width)
    cols = heads_here * (pair + pair // 2)
    return pl.pallas_call(
        functools.partial(project_kernel, heads_here),
        grid=(width // depth,),
        in_specs=[
            pl.BlockSpec((rows, depth), lambda i: (0, i)),
            pl.BlockSpec((depth, heads, pair), lambda i: (i, 0, 0)),
        ],
        out_specs=pl.BlockSpec((shards, rows, cols), lambda i: (0, 0, 0)),
        out_shape=jax.ShapeDtypeStruct((shards, rows, cols), jnp.bfloat16),
        scratch_shapes=[pltpu.VMEM((rows, heads * pair), jnp.float32)],
        cost_estimate=pl.CostEstimate(
            flops=2 * rows * width * heads * pair,
            bytes_accessed=2 * (rows * width + width * heads * pair + shards * rows * cols),
            transcendentals=0,
        ),
        name="project",
    )(tok_rows, kv_weight)


def attend_kernel(scale, x_ref, kv_ref, live_ref, grad_ref, mass_ref):
    heads = x_ref.shape[1]
    rows = x_ref.shape[2] // 2
    pair = x_ref.shape[3]
    head_dim = pair // 2
    last = (((1,), (1,)), ((), ()))
    live = live_ref[0] > 0.0
    mass = None
    for h in range(heads):
        x = x_ref[0, h]
        both = kv_ref[0, :, h * pair : (h + 1) * pair]
        start = heads * pair + h * head_dim
        low = kv_ref[0, :, start : start + head_dim]
        s = lax.dot_general(x, both, last, preferred_element_type=jnp.float32)
        s_low = lax.dot_general(
            x[:rows, :head_dim], low, last, preferred_element_type=jnp.float32
        )
        scores = jnp.where(live, (s[:rows] + s_low) * scale, -1e30)
        top = jnp.max(scores, axis=-1, keepdims=True)
        expo = jnp.where(live, jnp.exp(scores - top), 0.0)
        probs = expo / jnp.sum(expo, axis=-1, keepdims=True)
        probs_low = probs.astype(jnp.bfloat16)
        prob_grad = s[rows:]
        row_dot = jnp.sum(probs_low.astype(jnp.float32) * prob_grad, axis=-1, keepdims=True)
        score_grad = (probs * (prob_grad - row_dot) * scale).astype(jnp.bfloat16)
        y = jnp.concatenate([score_grad, probs_low], axis=0)
        pair_grad = lax.dot_general(
            y, x, (((0,), (0,)), ((), ())), preferred_element_type=jnp.float32
        )
        grad_ref[0, :, h * pair : (h + 1) * pair] = pair_grad.astype(jnp.bfloat16)
        part = jnp.sum(probs, axis=0, keepdims=True)
        mass = part if mass is None else mass + part
    mass_ref[0] = mass


def attend(x, kv, live, scale):
    count, heads, double_rows, pair = x.shape
    keys, cols = kv.shape[1:]
    return pl.pallas_call(
        functools.partial(attend_kernel, scale),
        grid=(count,),
        in_specs=[
            pl.BlockSpec((1, heads, double_rows, pair), lambda q: (q, 0, 0, 0)),
            pl.BlockSpec((1, keys, cols), lambda q: (q, 0, 0)),
            pl.BlockSpec((1, 1, keys), lambda q: (q, 0, 0)),
        ],
        out_specs=[
            pl.BlockSpec((1, keys, heads * pair), lambda q: (q, 0, 0)),
            pl.BlockSpec((1, 1, keys), lambda q: (q, 0, 0)),
        ],
        out_shape=[
            jax.ShapeDtypeStruct((count, keys, heads * pair), jnp.bfloat16),
            jax.ShapeDtypeStruct((count, 1, keys), jnp.float32),
        ],
        cost_estimate=pl.CostEstimate(
            flops=5 * count * heads * double_rows * keys * pair,
            bytes_accessed=2 * count * keys * (cols + heads * pair),
            transcendentals=count * heads * double_rows * keys // 2,
        ),
        name="attend",
    )(x, kv, live)


def spread_kernel(where_ref, piece_ref, out_ref):
    shards = piece_ref.shape[0]
    pair = out_ref.shape[2]
    heads_here = piece_ref.shape[2] // pair
    for j in range(shards):
        piece = piece_ref[where_ref[j]].astype(out_ref.dtype)
        for h in range(heads_here):
            out_ref[:, j * heads_here + h, :] = piece[:, h * pair : (h + 1) * pair]


def spread(pieces, where, pair):
    shards, rows, cols = pieces.shape
    heads = shards * cols // pair
    step = min(128, rows)
    return pl.pallas_call(
        spread_kernel,
        grid_spec=pltpu.PrefetchScalarGridSpec(
            num_scalar_prefetch=1,
            grid=(rows // step,),
            in_specs=[pl.BlockSpec((shards, step, cols), lambda i, w: (0, i, 0))],
            out_specs=pl.BlockSpec((step, heads, pair), lambda i, w: (i, 0, 0)),
        ),
        out_shape=jax.ShapeDtypeStruct((rows, heads, pair), jnp.bfloat16),
        cost_estimate=pl.CostEstimate(
            flops=0, bytes_accessed=4 * shards * rows * cols, transcendentals=0
        ),
        name="spread",
    )(where, pieces)


def wedge(left, right):
    return lax.dot_general(
        left, right, (((0,), (0,)), ((), ())), preferred_element_type=jnp.float32
    )


def on_device(
    enc_states,
    kv_weight,
    queries,
    out_grad,
    passage_order,
    passage_blocks,
    ret_tokens,
    ret_weight,
    question_emb,
):
    pass_dev = enc_states.shape[0]
    slot_len = enc_states.shape[2]
    width = enc_states.shape[3]
    pair_width = kv_weight.shape[2]
    heads_dec = kv_weight.shape[1]
    head_dim = pair_width // 2
    n_enc = lax.axis_size("enc")
    n_ret = lax.axis_size("ret")
    enc_rank = lax.axis_index("enc")
    dec_rank = lax.axis_index("dec")
    ret_rank = lax.axis_index("ret")
    order_row = passage_order[0]
    blocks_row = passage_blocks[0]
    group_pass = order_row.shape[0]
    question_count = queries.shape[0]
    query_len = queries.shape[1]
    heads_here = queries.shape[2]
    highest = lax.Precision.HIGHEST
    rows_dev = pass_dev * slot_len
    key_count = PASS * slot_len
    rows_group = group_pass * slot_len
    tok_rows = enc_states.reshape(rows_dev, width)

    sent = project(tok_rows, kv_weight, n_enc)
    kv = lax.all_to_all(sent, "enc", split_axis=0, concat_axis=0, tiled=True)
    cols = kv.shape[2]

    tok_cols = lax.all_to_all(tok_rows, "enc", split_axis=1, concat_axis=0, tiled=True)
    rows_out = width // (n_enc * n_ret)

    positions = jnp.arange(slot_len, dtype=jnp.int32)
    live_pass = (positions[None, :] < BLK * blocks_row[:, None]).astype(jnp.float32)
    chosen = order_row.reshape(question_count, PASS)
    if question_count == 1:
        kv = kv.reshape(1, key_count, cols)
        live = live_pass.reshape(1, 1, key_count)
    else:
        kv = kv.reshape(group_pass, slot_len, cols)[chosen].reshape(
            question_count, key_count, cols
        )
        live = live_pass[chosen].reshape(question_count, 1, key_count)
    query_t = jnp.transpose(queries, (0, 2, 1, 3))
    grad_t = jnp.transpose(out_grad, (0, 2, 1, 3))
    zero = jnp.zeros_like(query_t)
    x = jnp.concatenate(
        [
            jnp.concatenate([query_t, zero], axis=-1),
            jnp.concatenate([zero, grad_t], axis=-1),
        ],
        axis=2,
    )
    pair_grad, mass_keys = attend(x, kv, live, 1.0 / math.sqrt(head_dim))
    mass_part = mass_keys.reshape(question_count, PASS, slot_len).sum(axis=-1) / (
        HEADS * query_len
    )
    if question_count == 1:
        own_grad = pair_grad.reshape(rows_group, heads_here * pair_width)
        mass_part = mass_part[0][order_row][None]
    else:
        own_grad = (
            jnp.zeros((group_pass, slot_len, heads_here * pair_width), jnp.bfloat16)
            .at[order_row]
            .set(pair_grad.reshape(group_pass, slot_len, heads_here * pair_width))
            .reshape(rows_group, heads_here * pair_width)
        )

    half = rows_group // 2
    if n_enc == 4:
        flip = [[(i, i ^ bit) for i in range(n_enc)] for bit in (1, 2)]
        tops, bottoms = own_grad[:half], own_grad[half:]
        one_top = lax.ppermute(tops, "enc", flip[0])
        two_bottom = lax.ppermute(bottoms, "enc", flip[1])
        one_bottom = lax.ppermute(bottoms, "enc", flip[0])
        two_top = lax.ppermute(tops, "enc", flip[1])
        three_top = lax.ppermute(one_top, "enc", flip[1])
        three_bottom = lax.ppermute(two_bottom, "enc", flip[0])
        parts = [
            (tops, bottoms),
            (one_top, one_bottom),
            (two_top, two_bottom),
            (three_top, three_bottom),
        ]
        where = jnp.arange(n_enc, dtype=jnp.int32) ^ enc_rank
    else:
        gathered = lax.all_gather(own_grad, "enc", axis=0, tiled=False)
        parts = [(gathered[k][:half], gathered[k][half:]) for k in range(n_enc)]
        where = jnp.arange(n_enc, dtype=jnp.int32)

    def rows_of(rank):
        return lax.dynamic_slice_in_dim(tok_cols, rank * rows_out, rows_out, axis=1)

    own_sums = []
    own_cols = rows_of(ret_rank)
    other_cols = [rows_of((ret_rank + shift) % n_ret) for shift in range(1, n_ret)]
    for top, bottom in parts:
        piece = wedge(own_cols[:half], top) + wedge(own_cols[half:], bottom)
        for shift in range(1, n_ret):
            left = other_cols[shift - 1]
            away = (wedge(left[:half], top) + wedge(left[half:], bottom)).astype(jnp.bfloat16)
            got = lax.ppermute(away, "ret", [(i, (i + shift) % n_ret) for i in range(n_ret)])
            piece = piece + got.astype(jnp.float32)
        own_sums.append(piece.astype(jnp.bfloat16))
    weight_total = spread(jnp.stack(own_sums), where, pair_width)

    first_row = enc_rank * rows_dev
    mine = []
    for top, bottom in parts:
        in_top = lax.dynamic_slice_in_dim(top, jnp.minimum(first_row, half - rows_dev), rows_dev)
        in_bottom = lax.dynamic_slice_in_dim(
            bottom, jnp.maximum(first_row - half, 0), rows_dev
        )
        mine.append(jnp.where(first_row < half, in_top, in_bottom))
    kv_grad = spread(jnp.stack(mine), where, pair_width).reshape(
        pass_dev, 1, slot_len, heads_dec, pair_width
    )

    own_blocks = lax.dynamic_slice_in_dim(blocks_row, enc_rank * pass_dev, pass_dev)
    ret_rows = ret_tokens.reshape(pass_dev * slot_len, ret_tokens.shape[3])
    ret_width = ret_rows.shape[1]
    pre_act = jnp.dot(ret_rows, ret_weight, preferred_element_type=jnp.float32).reshape(
        pass_dev, slot_len, ret_width
    )
    hidden = jax.nn.gelu(pre_act)
    own_live = positions[None, :] < BLK * own_blocks[:, None]
    own_length = (BLK * own_blocks).astype(jnp.float32)
    embed_own = jnp.sum(jnp.where(own_live[..., None], hidden, 0.0), axis=1) / own_length[:, None]
    owner_map = (
        order_row[:, None] == enc_rank * pass_dev + jnp.arange(pass_dev, dtype=jnp.int32)[None, :]
    ).astype(jnp.float32)
    slot_embed = jnp.dot(owner_map, embed_own, precision=highest)
    emb_rep = jnp.repeat(question_emb, PASS, axis=0)
    score_part = jnp.sum(emb_rep * slot_embed, axis=-1) * (dec_rank == 0).astype(jnp.float32)
    passage_mass, ret_scores = lax.psum(
        (mass_part, score_part.reshape(question_count, PASS)), ("enc", "dec")
    )
    top_score = jnp.max(ret_scores, axis=-1, keepdims=True)
    expo_score = jnp.exp(ret_scores - top_score)
    score_gap = expo_score / jnp.sum(expo_score, axis=-1, keepdims=True) - passage_mass
    gap_rows = score_gap.reshape(-1, 1) * emb_rep
    embed_grad = jnp.dot(jnp.transpose(owner_map), gap_rows, precision=highest)
    hidden_grad = jnp.where(
        own_live[..., None], (embed_grad / own_length[:, None])[:, None, :], 0.0
    )
    pre_grad = gelu_grad(pre_act, hidden_grad).astype(jnp.bfloat16)
    ret_part_grad = wedge(ret_rows, pre_grad.reshape(-1, ret_width))
    ret_weight_grad = lax.psum(ret_part_grad.astype(jnp.bfloat16), ("enc", "ret"))
    return (kv_grad, weight_total, ret_weight_grad)


def solution(mesh):
    return jax.shard_map(
        on_device,
        mesh=mesh,
        in_specs=(
            P("enc", "ret", None, None),
            P(None, "dec", None),
            P("ret", None, ("dec", "enc"), None),
            P("ret", None, ("dec", "enc"), None),
            P("ret", None),
            P("ret", None),
            P("enc", "ret", None, None),
            P(),
            P("ret", None),
        ),
        out_specs=(P("enc", "ret", None, "dec", None), P(("enc", "ret"), "dec", None), P()),
        check_vma=False,
    )
```

```python
import functools
import math

import jax
import jax.numpy as jnp
from jax import lax
from jax.experimental import pallas as pl
from jax.experimental.pallas import tpu as pltpu
from jax.sharding import PartitionSpec as P

HEADS = 64
BLK = 128
PASS = 8


def gelu_grad(pre_act, upstream):
    return jax.vjp(jax.nn.gelu, pre_act)[1](upstream)[0]


def project_kernel(heads_here, x_ref, w_ref, out_ref, total, staged):
    step = pl.program_id(0)
    depth, heads, pair = w_ref.shape
    head_dim = pair // 2
    x = x_ref[...]
    staged[...] = w_ref[...].astype(jnp.float32).reshape(depth * heads, pair)
    for first in range(0, heads, 2):
        w_two = jnp.concatenate(
            [
                staged[pl.ds(first + k, depth, stride=heads), :].astype(jnp.bfloat16)
                for k in range(2)
            ],
            axis=-1,
        )
        part = jnp.dot(x, w_two, preferred_element_type=jnp.float32)
        cols = slice(first * pair, (first + 2) * pair)

        @pl.when(step == 0)
        def _():
            total[:, cols] = part

        @pl.when(step > 0)
        def _():
            total[:, cols] += part

    @pl.when(step == pl.num_programs(0) - 1)
    def _():
        for h in range(heads):
            dest, own = h // heads_here, h % heads_here
            wide = total[:, h * pair : (h + 1) * pair]
            high = wide.astype(jnp.bfloat16)
            low = (wide - high.astype(jnp.float32)).astype(jnp.bfloat16)
            out_ref[dest, :, own * pair : (own + 1) * pair] = high
            start = heads_here * pair + own * head_dim
            out_ref[dest, :, start : start + head_dim] = low[:, :head_dim]


def project(tok_rows, kv_weight, shards):
    rows, width = tok_rows.shape
    _, heads, pair = kv_weight.shape
    heads_here = heads // shards
    depth = min(512, width)
    cols = heads_here * (pair + pair // 2)
    return pl.pallas_call(
        functools.partial(project_kernel, heads_here),
        grid=(width // depth,),
        in_specs=[
            pl.BlockSpec((rows, depth), lambda i: (0, i)),
            pl.BlockSpec((depth, heads, pair), lambda i: (i, 0, 0)),
        ],
        out_specs=pl.BlockSpec((shards, rows, cols), lambda i: (0, 0, 0)),
        out_shape=jax.ShapeDtypeStruct((shards, rows, cols), jnp.bfloat16),
        scratch_shapes=[
            pltpu.VMEM((rows, heads * pair), jnp.float32),
            pltpu.VMEM((depth * heads, pair), jnp.float32),
        ],
        cost_estimate=pl.CostEstimate(
            flops=2 * rows * width * heads * pair,
            bytes_accessed=2 * (rows * width + width * heads * pair + shards * rows * cols),
            transcendentals=0,
        ),
        name="project",
    )(tok_rows, kv_weight)


def attend_kernel(scale, x_ref, kv_ref, live_ref, grad_ref, mass_ref):
    heads = x_ref.shape[1]
    rows = x_ref.shape[2] // 2
    pair = x_ref.shape[3]
    head_dim = pair // 2
    last = (((1,), (1,)), ((), ()))
    live = live_ref[0] > 0.0
    mass = None
    for h in range(heads):
        x = x_ref[0, h]
        both = kv_ref[0, :, h * pair : (h + 1) * pair]
        start = heads * pair + h * head_dim
        low = kv_ref[0, :, start : start + head_dim]
        s = lax.dot_general(x, both, last, preferred_element_type=jnp.float32)
        s_low = lax.dot_general(
            x[:rows, :head_dim], low, last, preferred_element_type=jnp.float32
        )
        scores = jnp.where(live, (s[:rows] + s_low) * scale, -1e30)
        top = jnp.max(scores, axis=-1, keepdims=True)
        expo = jnp.where(live, jnp.exp(scores - top), 0.0)
        probs = expo / jnp.sum(expo, axis=-1, keepdims=True)
        probs_low = probs.astype(jnp.bfloat16)
        prob_grad = s[rows:]
        row_dot = jnp.sum(probs_low.astype(jnp.float32) * prob_grad, axis=-1, keepdims=True)
        score_grad = (probs * (prob_grad - row_dot) * scale).astype(jnp.bfloat16)
        y = jnp.concatenate([score_grad, probs_low], axis=0)
        pair_grad = lax.dot_general(
            y, x, (((0,), (0,)), ((), ())), preferred_element_type=jnp.float32
        )
        grad_ref[0, :, h * pair : (h + 1) * pair] = pair_grad.astype(jnp.bfloat16)
        part = jnp.sum(probs, axis=0, keepdims=True)
        mass = part if mass is None else mass + part
    mass_ref[0] = mass


def attend(x, kv, live, scale):
    count, heads, double_rows, pair = x.shape
    keys, cols = kv.shape[1:]
    return pl.pallas_call(
        functools.partial(attend_kernel, scale),
        grid=(count,),
        in_specs=[
            pl.BlockSpec((1, heads, double_rows, pair), lambda q: (q, 0, 0, 0)),
            pl.BlockSpec((1, keys, cols), lambda q: (q, 0, 0)),
            pl.BlockSpec((1, 1, keys), lambda q: (q, 0, 0)),
        ],
        out_specs=[
            pl.BlockSpec((1, keys, heads * pair), lambda q: (q, 0, 0)),
            pl.BlockSpec((1, 1, keys), lambda q: (q, 0, 0)),
        ],
        out_shape=[
            jax.ShapeDtypeStruct((count, keys, heads * pair), jnp.bfloat16),
            jax.ShapeDtypeStruct((count, 1, keys), jnp.float32),
        ],
        cost_estimate=pl.CostEstimate(
            flops=5 * count * heads * double_rows * keys * pair,
            bytes_accessed=2 * count * keys * (cols + heads * pair),
            transcendentals=count * heads * double_rows * keys // 2,
        ),
        name="attend",
    )(x, kv, live)


def spread_kernel(where_ref, piece_ref, out_ref, staged):
    shards = piece_ref.shape[0]
    rows, heads, pair = out_ref.shape
    heads_here = heads // shards
    for j in range(shards):
        piece = piece_ref[where_ref[j]].astype(jnp.float32)
        for h in range(heads_here):
            staged[pl.ds(j * heads_here + h, rows, stride=heads), :] = piece[
                :, h * pair : (h + 1) * pair
            ]
    out_ref[...] = staged[...].reshape(rows, heads, pair).astype(out_ref.dtype)


def spread(pieces, where, pair):
    shards, rows, cols = pieces.shape
    heads = shards * cols // pair
    step = min(128, rows)
    return pl.pallas_call(
        spread_kernel,
        grid_spec=pltpu.PrefetchScalarGridSpec(
            num_scalar_prefetch=1,
            grid=(rows // step,),
            in_specs=[pl.BlockSpec((shards, step, cols), lambda i, w: (0, i, 0))],
            out_specs=pl.BlockSpec((step, heads, pair), lambda i, w: (i, 0, 0)),
            scratch_shapes=[pltpu.VMEM((step * heads, pair), jnp.float32)],
        ),
        out_shape=jax.ShapeDtypeStruct((rows, heads, pair), jnp.bfloat16),
        cost_estimate=pl.CostEstimate(
            flops=0, bytes_accessed=4 * shards * rows * cols, transcendentals=0
        ),
        name="spread",
    )(where, pieces)


def wedge(left, right):
    return lax.dot_general(
        left, right, (((0,), (0,)), ((), ())), preferred_element_type=jnp.float32
    )


def on_device(
    enc_states,
    kv_weight,
    queries,
    out_grad,
    passage_order,
    passage_blocks,
    ret_tokens,
    ret_weight,
    question_emb,
):
    pass_dev = enc_states.shape[0]
    slot_len = enc_states.shape[2]
    width = enc_states.shape[3]
    pair_width = kv_weight.shape[2]
    heads_dec = kv_weight.shape[1]
    head_dim = pair_width // 2
    n_enc = lax.axis_size("enc")
    n_ret = lax.axis_size("ret")
    enc_rank = lax.axis_index("enc")
    dec_rank = lax.axis_index("dec")
    ret_rank = lax.axis_index("ret")
    order_row = passage_order[0]
    blocks_row = passage_blocks[0]
    group_pass = order_row.shape[0]
    question_count = queries.shape[0]
    query_len = queries.shape[1]
    heads_here = queries.shape[2]
    highest = lax.Precision.HIGHEST
    rows_dev = pass_dev * slot_len
    key_count = PASS * slot_len
    tok_rows = enc_states.reshape(rows_dev, width)

    rows_out = width // (n_enc * n_ret)
    rows_group = group_pass * slot_len
    split_cols = tok_rows.reshape(rows_dev, n_enc, n_ret, rows_out)

    def columns_of(rank):
        block = lax.dynamic_index_in_dim(split_cols, rank, axis=2, keepdims=False)
        block = jnp.transpose(block, (1, 0, 2))
        return lax.all_to_all(block, "enc", split_axis=0, concat_axis=0, tiled=True).reshape(
            rows_group, rows_out
        )

    own_cols = columns_of(ret_rank)

    sent = project(tok_rows, kv_weight, n_enc)
    kv = lax.all_to_all(sent, "enc", split_axis=0, concat_axis=0, tiled=True)
    cols = kv.shape[2]
    other_cols = [columns_of((ret_rank + shift) % n_ret) for shift in range(1, n_ret)]

    positions = jnp.arange(slot_len, dtype=jnp.int32)
    live_pass = (positions[None, :] < BLK * blocks_row[:, None]).astype(jnp.float32)
    chosen = order_row.reshape(question_count, PASS)
    if question_count == 1:
        kv = kv.reshape(1, key_count, cols)
        live = live_pass.reshape(1, 1, key_count)
    else:
        kv = kv.reshape(group_pass, slot_len, cols)[chosen].reshape(
            question_count, key_count, cols
        )
        live = live_pass[chosen].reshape(question_count, 1, key_count)
    query_t = jnp.transpose(queries, (0, 2, 1, 3))
    grad_t = jnp.transpose(out_grad, (0, 2, 1, 3))
    zero = jnp.zeros_like(query_t)
    x = jnp.concatenate(
        [
            jnp.concatenate([query_t, zero], axis=-1),
            jnp.concatenate([zero, grad_t], axis=-1),
        ],
        axis=2,
    )
    pair_grad, mass_keys = attend(x, kv, live, 1.0 / math.sqrt(head_dim))
    mass_part = mass_keys.reshape(question_count, PASS, slot_len).sum(axis=-1) / (
        HEADS * query_len
    )
    if question_count == 1:
        own_grad = pair_grad.reshape(rows_group, heads_here * pair_width)
        mass_part = mass_part[0][order_row][None]
    else:
        own_grad = (
            jnp.zeros((group_pass, slot_len, heads_here * pair_width), jnp.bfloat16)
            .at[order_row]
            .set(pair_grad.reshape(group_pass, slot_len, heads_here * pair_width))
            .reshape(rows_group, heads_here * pair_width)
        )

    own_blocks = lax.dynamic_slice_in_dim(blocks_row, enc_rank * pass_dev, pass_dev)
    ret_rows = ret_tokens.reshape(pass_dev * slot_len, ret_tokens.shape[3])
    ret_width = ret_rows.shape[1]
    pre_act = jnp.dot(ret_rows, ret_weight, preferred_element_type=jnp.float32).reshape(
        pass_dev, slot_len, ret_width
    )
    hidden = jax.nn.gelu(pre_act)
    own_live = positions[None, :] < BLK * own_blocks[:, None]
    own_length = (BLK * own_blocks).astype(jnp.float32)
    embed_own = jnp.sum(jnp.where(own_live[..., None], hidden, 0.0), axis=1) / own_length[:, None]
    owner_map = (
        order_row[:, None] == enc_rank * pass_dev + jnp.arange(pass_dev, dtype=jnp.int32)[None, :]
    ).astype(jnp.float32)
    slot_embed = jnp.dot(owner_map, embed_own, precision=highest)
    emb_rep = jnp.repeat(question_emb, PASS, axis=0)
    score_part = jnp.sum(emb_rep * slot_embed, axis=-1) * (dec_rank == 0).astype(jnp.float32)
    passage_mass, ret_scores = lax.psum(
        (mass_part, score_part.reshape(question_count, PASS)), ("enc", "dec")
    )
    own_grad, passage_mass, ret_scores = lax.optimization_barrier(
        (own_grad, passage_mass, ret_scores)
    )

    half = rows_group // 2
    if n_enc == 4:
        flip = [[(i, i ^ bit) for i in range(n_enc)] for bit in (1, 2)]
        tops, bottoms = own_grad[:half], own_grad[half:]
        one_top = lax.ppermute(tops, "enc", flip[0])
        two_bottom = lax.ppermute(bottoms, "enc", flip[1])
        one_bottom = lax.ppermute(bottoms, "enc", flip[0])
        two_top = lax.ppermute(tops, "enc", flip[1])
        three_top = lax.ppermute(one_top, "enc", flip[1])
        three_bottom = lax.ppermute(two_bottom, "enc", flip[0])
        parts = [
            (tops, bottoms),
            (one_top, one_bottom),
            (two_top, two_bottom),
            (three_top, three_bottom),
        ]
        where = jnp.arange(n_enc, dtype=jnp.int32) ^ enc_rank
    else:
        gathered = lax.all_gather(own_grad, "enc", axis=0, tiled=False)
        parts = [(gathered[k][:half], gathered[k][half:]) for k in range(n_enc)]
        where = jnp.arange(n_enc, dtype=jnp.int32)

    own_sums = []
    for top, bottom in parts:
        piece = wedge(own_cols[:half], top) + wedge(own_cols[half:], bottom)
        for shift in range(1, n_ret):
            left = other_cols[shift - 1]
            away = (wedge(left[:half], top) + wedge(left[half:], bottom)).astype(jnp.bfloat16)
            got = lax.ppermute(away, "ret", [(i, (i + shift) % n_ret) for i in range(n_ret)])
            piece = piece + got.astype(jnp.float32)
        own_sums.append(piece.astype(jnp.bfloat16))
    weight_total = spread(jnp.stack(own_sums), where, pair_width)

    first_row = enc_rank * rows_dev
    mine = []
    for top, bottom in parts:
        in_top = lax.dynamic_slice_in_dim(top, jnp.minimum(first_row, half - rows_dev), rows_dev)
        in_bottom = lax.dynamic_slice_in_dim(
            bottom, jnp.maximum(first_row - half, 0), rows_dev
        )
        mine.append(jnp.where(first_row < half, in_top, in_bottom))
    kv_grad = spread(jnp.stack(mine), where, pair_width).reshape(
        pass_dev, 1, slot_len, heads_dec, pair_width
    )

    top_score = jnp.max(ret_scores, axis=-1, keepdims=True)
    expo_score = jnp.exp(ret_scores - top_score)
    score_gap = expo_score / jnp.sum(expo_score, axis=-1, keepdims=True) - passage_mass
    gap_rows = score_gap.reshape(-1, 1) * emb_rep
    embed_grad = jnp.dot(jnp.transpose(owner_map), gap_rows, precision=highest)
    hidden_grad = jnp.where(
        own_live[..., None], (embed_grad / own_length[:, None])[:, None, :], 0.0
    )
    pre_grad = gelu_grad(pre_act, hidden_grad).astype(jnp.bfloat16)
    ret_part_grad = wedge(ret_rows, pre_grad.reshape(-1, ret_width))
    ret_weight_grad = lax.psum(ret_part_grad.astype(jnp.bfloat16), ("enc", "ret"))
    return (kv_grad, weight_total, ret_weight_grad)


def solution(mesh):
    return jax.shard_map(
        on_device,
        mesh=mesh,
        in_specs=(
            P("enc", "ret", None, None),
            P(None, "dec", None),
            P("ret", None, ("dec", "enc"), None),
            P("ret", None, ("dec", "enc"), None),
            P("ret", None),
            P("ret", None),
            P("enc", "ret", None, None),
            P(),
            P("ret", None),
        ),
        out_specs=(P("enc", "ret", None, "dec", None), P(("enc", "ret"), "dec", None), P()),
        check_vma=False,
    )
```

```python
import functools
import math

import jax
import jax.numpy as jnp
from jax import lax
from jax.experimental import pallas as pl
from jax.experimental.pallas import tpu as pltpu
from jax.sharding import PartitionSpec as P

HEADS = 64
BLK = 128
PASS = 8


def gelu_grad(pre_act, upstream):
    return jax.vjp(jax.nn.gelu, pre_act)[1](upstream)[0]


def project_kernel(heads_here, x_ref, w_ref, out_ref, total, staged):
    step = pl.program_id(0)
    depth, heads, pair = w_ref.shape
    head_dim = pair // 2
    x = x_ref[...]
    staged[...] = w_ref[...].astype(jnp.float32).reshape(depth * heads, pair)
    for first in range(0, heads, 2):
        w_two = jnp.concatenate(
            [
                staged[pl.ds(first + k, depth, stride=heads), :].astype(jnp.bfloat16)
                for k in range(2)
            ],
            axis=-1,
        )
        part = jnp.dot(x, w_two, preferred_element_type=jnp.float32)
        cols = slice(first * pair, (first + 2) * pair)

        @pl.when(step == 0)
        def _():
            total[:, cols] = part

        @pl.when(step > 0)
        def _():
            total[:, cols] += part

    @pl.when(step == pl.num_programs(0) - 1)
    def _():
        for h in range(heads):
            dest, own = h // heads_here, h % heads_here
            wide = total[:, h * pair : (h + 1) * pair]
            high = wide.astype(jnp.bfloat16)
            low = (wide - high.astype(jnp.float32)).astype(jnp.bfloat16)
            out_ref[dest, :, own * pair : (own + 1) * pair] = high
            start = heads_here * pair + own * head_dim
            out_ref[dest, :, start : start + head_dim] = low[:, :head_dim]


def project(tok_rows, kv_weight, shards):
    rows, width = tok_rows.shape
    _, heads, pair = kv_weight.shape
    heads_here = heads // shards
    depth = min(512, width)
    cols = heads_here * (pair + pair // 2)
    return pl.pallas_call(
        functools.partial(project_kernel, heads_here),
        grid=(width // depth,),
        in_specs=[
            pl.BlockSpec((rows, depth), lambda i: (0, i)),
            pl.BlockSpec((depth, heads, pair), lambda i: (i, 0, 0)),
        ],
        out_specs=pl.BlockSpec((shards, rows, cols), lambda i: (0, 0, 0)),
        out_shape=jax.ShapeDtypeStruct((shards, rows, cols), jnp.bfloat16),
        scratch_shapes=[
            pltpu.VMEM((rows, heads * pair), jnp.float32),
            pltpu.VMEM((depth * heads, pair), jnp.float32),
        ],
        cost_estimate=pl.CostEstimate(
            flops=2 * rows * width * heads * pair,
            bytes_accessed=2 * (rows * width + width * heads * pair + shards * rows * cols),
            transcendentals=0,
        ),
        name="project",
    )(tok_rows, kv_weight)


def attend_kernel(scale, x_ref, kv_ref, live_ref, grad_ref, mass_ref):
    heads = x_ref.shape[1]
    rows = x_ref.shape[2] // 2
    pair = x_ref.shape[3]
    head_dim = pair // 2
    last = (((1,), (1,)), ((), ()))
    live = live_ref[0] > 0.0
    mass = None
    for h in range(heads):
        x = x_ref[0, h]
        both = kv_ref[0, :, h * pair : (h + 1) * pair]
        start = heads * pair + h * head_dim
        low = kv_ref[0, :, start : start + head_dim]
        s = lax.dot_general(x, both, last, preferred_element_type=jnp.float32)
        s_low = lax.dot_general(
            x[:rows, :head_dim], low, last, preferred_element_type=jnp.float32
        )
        scores = jnp.where(live, (s[:rows] + s_low) * scale, -1e30)
        top = jnp.max(scores, axis=-1, keepdims=True)
        expo = jnp.where(live, jnp.exp(scores - top), 0.0)
        probs = expo / jnp.sum(expo, axis=-1, keepdims=True)
        probs_low = probs.astype(jnp.bfloat16)
        prob_grad = s[rows:]
        row_dot = jnp.sum(probs_low.astype(jnp.float32) * prob_grad, axis=-1, keepdims=True)
        score_grad = (probs * (prob_grad - row_dot) * scale).astype(jnp.bfloat16)
        y = jnp.concatenate([score_grad, probs_low], axis=0)
        pair_grad = lax.dot_general(
            y, x, (((0,), (0,)), ((), ())), preferred_element_type=jnp.float32
        )
        grad_ref[0, :, h * pair : (h + 1) * pair] = pair_grad.astype(jnp.bfloat16)
        part = jnp.sum(probs, axis=0, keepdims=True)
        mass = part if mass is None else mass + part
    mass_ref[0] = mass


def attend(x, kv, live, scale):
    count, heads, double_rows, pair = x.shape
    keys, cols = kv.shape[1:]
    return pl.pallas_call(
        functools.partial(attend_kernel, scale),
        grid=(count,),
        in_specs=[
            pl.BlockSpec((1, heads, double_rows, pair), lambda q: (q, 0, 0, 0)),
            pl.BlockSpec((1, keys, cols), lambda q: (q, 0, 0)),
            pl.BlockSpec((1, 1, keys), lambda q: (q, 0, 0)),
        ],
        out_specs=[
            pl.BlockSpec((1, keys, heads * pair), lambda q: (q, 0, 0)),
            pl.BlockSpec((1, 1, keys), lambda q: (q, 0, 0)),
        ],
        out_shape=[
            jax.ShapeDtypeStruct((count, keys, heads * pair), jnp.bfloat16),
            jax.ShapeDtypeStruct((count, 1, keys), jnp.float32),
        ],
        cost_estimate=pl.CostEstimate(
            flops=5 * count * heads * double_rows * keys * pair,
            bytes_accessed=2 * count * keys * (cols + heads * pair),
            transcendentals=count * heads * double_rows * keys // 2,
        ),
        name="attend",
    )(x, kv, live)


def spread_kernel(where_ref, piece_ref, out_ref, staged):
    shards = piece_ref.shape[0]
    rows, heads, pair = out_ref.shape
    heads_here = heads // shards
    for j in range(shards):
        piece = piece_ref[where_ref[j]].astype(jnp.float32)
        for h in range(heads_here):
            staged[pl.ds(j * heads_here + h, rows, stride=heads), :] = piece[
                :, h * pair : (h + 1) * pair
            ]
    out_ref[...] = staged[...].reshape(rows, heads, pair).astype(out_ref.dtype)


def spread(pieces, where, pair):
    shards, rows, cols = pieces.shape
    heads = shards * cols // pair
    step = min(128, rows)
    return pl.pallas_call(
        spread_kernel,
        grid_spec=pltpu.PrefetchScalarGridSpec(
            num_scalar_prefetch=1,
            grid=(rows // step,),
            in_specs=[pl.BlockSpec((shards, step, cols), lambda i, w: (0, i, 0))],
            out_specs=pl.BlockSpec((step, heads, pair), lambda i, w: (i, 0, 0)),
            scratch_shapes=[pltpu.VMEM((step * heads, pair), jnp.float32)],
        ),
        out_shape=jax.ShapeDtypeStruct((rows, heads, pair), jnp.bfloat16),
        cost_estimate=pl.CostEstimate(
            flops=0, bytes_accessed=4 * shards * rows * cols, transcendentals=0
        ),
        name="spread",
    )(where, pieces)


def wedge(left, right):
    return lax.dot_general(
        left, right, (((0,), (0,)), ((), ())), preferred_element_type=jnp.float32
    )


def sum_over(value, axes):
    for axis in axes:
        size = lax.axis_size(axis)
        if size & (size - 1):
            value = lax.psum(value, axis)
            continue
        bit = 1
        while bit < size:
            value = value + lax.ppermute(value, axis, [(i, i ^ bit) for i in range(size)])
            bit *= 2
    return value


def on_device(
    enc_states,
    kv_weight,
    queries,
    out_grad,
    passage_order,
    passage_blocks,
    ret_tokens,
    ret_weight,
    question_emb,
):
    pass_dev = enc_states.shape[0]
    slot_len = enc_states.shape[2]
    width = enc_states.shape[3]
    pair_width = kv_weight.shape[2]
    heads_dec = kv_weight.shape[1]
    head_dim = pair_width // 2
    n_enc = lax.axis_size("enc")
    n_ret = lax.axis_size("ret")
    enc_rank = lax.axis_index("enc")
    dec_rank = lax.axis_index("dec")
    ret_rank = lax.axis_index("ret")
    order_row = passage_order[0]
    blocks_row = passage_blocks[0]
    group_pass = order_row.shape[0]
    question_count = queries.shape[0]
    query_len = queries.shape[1]
    heads_here = queries.shape[2]
    highest = lax.Precision.HIGHEST
    rows_dev = pass_dev * slot_len
    key_count = PASS * slot_len
    tok_rows = enc_states.reshape(rows_dev, width)

    rows_out = width // (n_enc * n_ret)
    rows_group = group_pass * slot_len

    def columns_of(rank):
        blocks = []
        for j in range(n_enc):
            first = j * n_ret * rows_out
            block = tok_rows[:, first : first + rows_out]
            for k in range(1, n_ret):
                start = first + k * rows_out
                block = jnp.where(rank == k, tok_rows[:, start : start + rows_out], block)
            blocks.append(block)
        block = jnp.stack(blocks)
        return lax.all_to_all(block, "enc", split_axis=0, concat_axis=0, tiled=True).reshape(
            rows_group, rows_out
        )

    own_cols = columns_of(ret_rank)

    sent = project(tok_rows, kv_weight, n_enc)
    kv = lax.all_to_all(sent, "enc", split_axis=0, concat_axis=0, tiled=True)
    cols = kv.shape[2]
    other_cols = [columns_of((ret_rank + shift) % n_ret) for shift in range(1, n_ret)]

    positions = jnp.arange(slot_len, dtype=jnp.int32)
    live_pass = (positions[None, :] < BLK * blocks_row[:, None]).astype(jnp.float32)
    chosen = order_row.reshape(question_count, PASS)
    if question_count == 1:
        kv = kv.reshape(1, key_count, cols)
        live = live_pass.reshape(1, 1, key_count)
    else:
        kv = kv.reshape(group_pass, slot_len, cols)[chosen].reshape(
            question_count, key_count, cols
        )
        live = live_pass[chosen].reshape(question_count, 1, key_count)
    query_t = jnp.transpose(queries, (0, 2, 1, 3))
    grad_t = jnp.transpose(out_grad, (0, 2, 1, 3))
    zero = jnp.zeros_like(query_t)
    x = jnp.concatenate(
        [
            jnp.concatenate([query_t, zero], axis=-1),
            jnp.concatenate([zero, grad_t], axis=-1),
        ],
        axis=2,
    )
    pair_grad, mass_keys = attend(x, kv, live, 1.0 / math.sqrt(head_dim))
    mass_part = mass_keys.reshape(question_count, PASS, slot_len).sum(axis=-1) / (
        HEADS * query_len
    )
    if question_count == 1:
        own_grad = pair_grad.reshape(rows_group, heads_here * pair_width)
        mass_part = mass_part[0][order_row][None]
    else:
        own_grad = (
            jnp.zeros((group_pass, slot_len, heads_here * pair_width), jnp.bfloat16)
            .at[order_row]
            .set(pair_grad.reshape(group_pass, slot_len, heads_here * pair_width))
            .reshape(rows_group, heads_here * pair_width)
        )

    own_blocks = lax.dynamic_slice_in_dim(blocks_row, enc_rank * pass_dev, pass_dev)
    ret_rows = ret_tokens.reshape(pass_dev * slot_len, ret_tokens.shape[3])
    ret_width = ret_rows.shape[1]
    pre_act = jnp.dot(ret_rows, ret_weight, preferred_element_type=jnp.float32).reshape(
        pass_dev, slot_len, ret_width
    )
    hidden = jax.nn.gelu(pre_act)
    own_live = positions[None, :] < BLK * own_blocks[:, None]
    own_length = (BLK * own_blocks).astype(jnp.float32)
    embed_own = jnp.sum(jnp.where(own_live[..., None], hidden, 0.0), axis=1) / own_length[:, None]
    owner_map = (
        order_row[:, None] == enc_rank * pass_dev + jnp.arange(pass_dev, dtype=jnp.int32)[None, :]
    ).astype(jnp.float32)
    slot_embed = jnp.dot(owner_map, embed_own, precision=highest)
    emb_rep = jnp.repeat(question_emb, PASS, axis=0)
    score_part = jnp.sum(emb_rep * slot_embed, axis=-1) * (dec_rank == 0).astype(jnp.float32)
    passage_mass, ret_scores = sum_over(
        jnp.stack([mass_part, score_part.reshape(question_count, PASS)]), ("enc", "dec")
    )
    own_grad, passage_mass, ret_scores = lax.optimization_barrier(
        (own_grad, passage_mass, ret_scores)
    )

    half = rows_group // 2
    if n_enc == 4:
        flip = [[(i, i ^ bit) for i in range(n_enc)] for bit in (1, 2)]
        tops, bottoms = own_grad[:half], own_grad[half:]
        one_top = lax.ppermute(tops, "enc", flip[0])
        two_bottom = lax.ppermute(bottoms, "enc", flip[1])
        one_bottom = lax.ppermute(bottoms, "enc", flip[0])
        two_top = lax.ppermute(tops, "enc", flip[1])
        three_top = lax.ppermute(one_top, "enc", flip[1])
        three_bottom = lax.ppermute(two_bottom, "enc", flip[0])
        parts = [
            (tops, bottoms),
            (one_top, one_bottom),
            (two_top, two_bottom),
            (three_top, three_bottom),
        ]
        where = jnp.arange(n_enc, dtype=jnp.int32) ^ enc_rank
    else:
        gathered = lax.all_gather(own_grad, "enc", axis=0, tiled=False)
        parts = [(gathered[k][:half], gathered[k][half:]) for k in range(n_enc)]
        where = jnp.arange(n_enc, dtype=jnp.int32)

    own_sums = []
    for top, bottom in parts:
        piece = wedge(own_cols[:half], top) + wedge(own_cols[half:], bottom)
        for shift in range(1, n_ret):
            left = other_cols[shift - 1]
            away = (wedge(left[:half], top) + wedge(left[half:], bottom)).astype(jnp.bfloat16)
            got = lax.ppermute(away, "ret", [(i, (i + shift) % n_ret) for i in range(n_ret)])
            piece = piece + got.astype(jnp.float32)
        own_sums.append(piece.astype(jnp.bfloat16))
    weight_total = spread(jnp.stack(own_sums), where, pair_width)

    first_row = enc_rank * rows_dev
    mine = []
    for top, bottom in parts:
        in_top = lax.dynamic_slice_in_dim(top, jnp.minimum(first_row, half - rows_dev), rows_dev)
        in_bottom = lax.dynamic_slice_in_dim(
            bottom, jnp.maximum(first_row - half, 0), rows_dev
        )
        mine.append(jnp.where(first_row < half, in_top, in_bottom))
    kv_grad = spread(jnp.stack(mine), where, pair_width).reshape(
        pass_dev, 1, slot_len, heads_dec, pair_width
    )

    top_score = jnp.max(ret_scores, axis=-1, keepdims=True)
    expo_score = jnp.exp(ret_scores - top_score)
    score_gap = expo_score / jnp.sum(expo_score, axis=-1, keepdims=True) - passage_mass
    gap_rows = score_gap.reshape(-1, 1) * emb_rep
    embed_grad = jnp.dot(jnp.transpose(owner_map), gap_rows, precision=highest)
    hidden_grad = jnp.where(
        own_live[..., None], (embed_grad / own_length[:, None])[:, None, :], 0.0
    )
    pre_grad = gelu_grad(pre_act, hidden_grad).astype(jnp.bfloat16)
    ret_part_grad = wedge(ret_rows, pre_grad.reshape(-1, ret_width))
    ret_weight_grad = lax.psum(ret_part_grad.astype(jnp.bfloat16), ("enc", "ret"))
    return (kv_grad, weight_total, ret_weight_grad)


def solution(mesh):
    return jax.shard_map(
        on_device,
        mesh=mesh,
        in_specs=(
            P("enc", "ret", None, None),
            P(None, "dec", None),
            P("ret", None, ("dec", "enc"), None),
            P("ret", None, ("dec", "enc"), None),
            P("ret", None),
            P("ret", None),
            P("enc", "ret", None, None),
            P(),
            P("ret", None),
        ),
        out_specs=(P("enc", "ret", None, "dec", None), P(("enc", "ret"), "dec", None), P()),
        check_vma=False,
    )
```
